32 devices in a mesh: gx: 4 (over y, x), gy: 2 (over core), vert: 4 (over z).
Axes of the slice: x: 2, y: 2, z: 4, core: 2. Of those that a mesh axis runs over, the one named last changes fastest.
Arguments:
- distribution: float32 [256, 64, 4096], P('gx', 'gy', 'vert'), as said below
- solid_mask: int32 [256, 64], P('gx', 'gy'), may hold values from 0 to 1, as said below
- normal_code: int32 [256, 64], P('gx', 'gy'), may hold values from 0 to 3
Outputs:
- new_field: float32 [256, 64, 4096], P('gx', 'gy', 'vert')
The draws below stay inside these ranges and needn't reach their ends.
Inputs may be any that keep to these rules, and one draw needn't show every extreme that they name: distribution is positive. `solid_mask`: no solid cell lies in the first or last row or column of an aligned block of 64 x 32 cells.
All inputs are finite; a program needn't handle non-finite values.
Results may differ from the reference program's by a relative error of at most 0.0001.
Values sent between devices are 32-bit elements; how exact they have to be, the bound alone decides.
A program may use at most 128 MiB of HBM per device.

```python
import math
import jax
import jax.numpy as jnp
from jax import lax

CX = 64
CY = 32
NVEL = 16
STEPS = 3
GRID_ROWS_LEADING = 256
GRID_COLS_TRAILING = 64
NV = 4096


def draw_distribution(key, part):
    stochastic_seeds = jax.random.split(key, 4)
    discrete_speed_total = NVEL
    mesh_step_width = 12.0 / discrete_speed_total
    centre = (discrete_speed_total - 1) / 2.0
    vel_index = jnp.arange(NV, dtype=jnp.int32)
    discrete_speed_east = (vel_index // discrete_speed_total % discrete_speed_total).astype(jnp.float32) * mesh_step_width - centre * mesh_step_width
    discrete_speed_north = (vel_index % discrete_speed_total).astype(jnp.float32) * mesh_step_width - centre * mesh_step_width
    discrete_speed_upward = (vel_index // (discrete_speed_total * discrete_speed_total)).astype(jnp.float32) * mesh_step_width - centre * mesh_step_width
    particle_concentration = jnp.exp(jax.random.uniform(stochastic_seeds[0], (GRID_ROWS_LEADING, GRID_COLS_TRAILING, 1), jnp.float32, math.log(0.5), math.log(2.0)))
    flow = jax.random.uniform(stochastic_seeds[1], (GRID_ROWS_LEADING, GRID_COLS_TRAILING, 3), jnp.float32, -1.5, 1.5)
    site_heat_level = jnp.exp(jax.random.uniform(stochastic_seeds[2], (GRID_ROWS_LEADING, GRID_COLS_TRAILING, 1), jnp.float32, math.log(2.0), math.log(8.0)))
    noise = jax.random.uniform(stochastic_seeds[3], (GRID_ROWS_LEADING, GRID_COLS_TRAILING, NV), jnp.float32, 0.5, 1.5)
    offset_x = discrete_speed_east - flow[:, :, 0:1]
    offset_y = discrete_speed_north - flow[:, :, 1:2]
    offset_z = discrete_speed_upward - flow[:, :, 2:3]
    maxwellian_width_sigma = offset_x * offset_x + offset_y * offset_y + offset_z * offset_z
    maxwellian_shape = jnp.exp(-maxwellian_width_sigma / (2.0 * site_heat_level)) + 0.2
    return particle_concentration * maxwellian_shape * noise


def draw_solid_mask(key, part):
    row_pos = jnp.arange(GRID_ROWS_LEADING, dtype=jnp.int32)[:, None] % CX
    col_pos = jnp.arange(GRID_COLS_TRAILING, dtype=jnp.int32)[None, :] % CY
    inner = (row_pos >= 1) & (row_pos <= CX - 2) & (col_pos >= 1) & (col_pos <= CY - 2)
    picked = jax.random.randint(key, (GRID_ROWS_LEADING, GRID_COLS_TRAILING), 0, 6) == 0
    return jnp.where(inner & picked, 1, 0).astype(jnp.int32)


def set_ends(values, stream_key, least, high):
    longest = values.shape.index(max(values.shape))
    spots = []
    for shift in (0, 1):
        where = [jax.random.randint(jax.random.fold_in(stream_key, axis), (), 0, length) for axis, length in enumerate(values.shape)]
        where[longest] = (where[longest] + shift) % values.shape[longest]
        spots.append(tuple(where))
    return values.at[spots[0]].set(least).at[spots[1]].set(high)


def setup_inputs(seed: int = 0) -> dict:
    seeds = jax.random.split(jax.random.key(seed), 4)
    return {
        "distribution": draw_distribution(jax.random.fold_in(seeds[3], 71), 0),
        "solid_mask": draw_solid_mask(jax.random.fold_in(seeds[3], 71), 0),
        "normal_code": set_ends(jax.random.randint(seeds[2], (GRID_ROWS_LEADING, GRID_COLS_TRAILING), 0, 4), jax.random.fold_in(seeds[2], 1), 0, 3).astype(jnp.int32),
    }


velocity_span = 12.0
courant = 0.08
collision_rate_inverse_tau = 2.0
wall_heat_level = 3.0


def velocity_parts(vel_index, discrete_speed_total):
    mesh_step_width = velocity_span / discrete_speed_total
    centre = (discrete_speed_total - 1) / 2.0
    plane_z = vel_index // (discrete_speed_total * discrete_speed_total)
    plane_x = (vel_index // discrete_speed_total) % discrete_speed_total
    plane_y = vel_index % discrete_speed_total
    return ((plane_x.astype(jnp.float32) - centre) * mesh_step_width,
            (plane_y.astype(jnp.float32) - centre) * mesh_step_width,
            (plane_z.astype(jnp.float32) - centre) * mesh_step_width)


def wall_shape(discrete_speed_east, discrete_speed_north, discrete_speed_upward, discrete_speed_total):
    mesh_step_width = velocity_span / discrete_speed_total
    normalising_coefficient = mesh_step_width ** 3 * (2.0 * math.pi * wall_heat_level) ** -1.5
    return normalising_coefficient * jnp.exp(-(discrete_speed_east * discrete_speed_east + discrete_speed_north * discrete_speed_north + discrete_speed_upward * discrete_speed_upward) / (2.0 * wall_heat_level))


def wall_weights(discrete_speed_east, discrete_speed_north):
    return jnp.stack([jnp.maximum(-discrete_speed_east, 0.0), jnp.maximum(discrete_speed_east, 0.0),
                      jnp.maximum(-discrete_speed_north, 0.0), jnp.maximum(discrete_speed_north, 0.0)], axis=1)


def moment_table(discrete_speed_east, discrete_speed_north, discrete_speed_upward):
    return jnp.stack([jnp.ones_like(discrete_speed_east), discrete_speed_east, discrete_speed_north, discrete_speed_upward,
                      discrete_speed_east * discrete_speed_east + discrete_speed_north * discrete_speed_north + discrete_speed_upward * discrete_speed_upward], axis=1)


def neighbor_flux(partial_value, normal_code):
    from_plus_x = jnp.roll(partial_value[:, :, 0], -1, axis=0)
    from_minus_x = jnp.roll(partial_value[:, :, 1], 1, axis=0)
    from_plus_y = jnp.roll(partial_value[:, :, 2], -1, axis=1)
    from_minus_y = jnp.roll(partial_value[:, :, 3], 1, axis=1)
    return jnp.where(normal_code == 0, from_plus_x,
                     jnp.where(normal_code == 1, from_minus_x,
                               jnp.where(normal_code == 2, from_plus_y, from_minus_y)))


def transport(center, left_side, right_side, down_side, up_side, discrete_speed_east, discrete_speed_north):
    return center - courant * (jnp.maximum(discrete_speed_east, 0.0) * (center - left_side)
                               + jnp.minimum(discrete_speed_east, 0.0) * (right_side - center)
                               + jnp.maximum(discrete_speed_north, 0.0) * (center - down_side)
                               + jnp.minimum(discrete_speed_north, 0.0) * (up_side - center))


def relax_cells(moved, aggregated_integrals, discrete_speed_east, discrete_speed_north, discrete_speed_upward, discrete_speed_total):
    particle_concentration = aggregated_integrals[:, 0:1]
    mean_drift_east = aggregated_integrals[:, 1:2] / particle_concentration
    mean_drift_north = aggregated_integrals[:, 2:3] / particle_concentration
    mean_drift_upward = aggregated_integrals[:, 3:4] / particle_concentration
    site_heat_level = (aggregated_integrals[:, 4:5] / particle_concentration - (mean_drift_east * mean_drift_east + mean_drift_north * mean_drift_north + mean_drift_upward * mean_drift_upward)) / 3.0
    mesh_step_width = velocity_span / discrete_speed_total
    offset_x = discrete_speed_east - mean_drift_east
    offset_y = discrete_speed_north - mean_drift_north
    offset_z = discrete_speed_upward - mean_drift_upward
    maxwellian_width_sigma = offset_x * offset_x + offset_y * offset_y + offset_z * offset_z
    maxwellian_target = particle_concentration * mesh_step_width ** 3 * (2.0 * math.pi * site_heat_level) ** -1.5 * jnp.exp(-maxwellian_width_sigma / (2.0 * site_heat_level))
    collision_decay_factor = collision_rate_inverse_tau * particle_concentration / (discrete_speed_total ** 3) * site_heat_level ** 0.28
    return (moved + collision_decay_factor * maxwellian_target) / (1.0 + collision_decay_factor)


def reference(distribution, solid_mask, normal_code):
    discrete_speed_total = NVEL
    plane_size = discrete_speed_total * discrete_speed_total
    cells = GRID_ROWS_LEADING * GRID_COLS_TRAILING
    vel_index = jnp.arange(NV, dtype=jnp.int32)
    discrete_speed_east, discrete_speed_north, discrete_speed_upward = velocity_parts(vel_index, discrete_speed_total)
    shape_all = wall_shape(discrete_speed_east, discrete_speed_north, discrete_speed_upward, discrete_speed_total)
    wall_norm = jnp.sum(shape_all * jnp.maximum(discrete_speed_east, 0.0))
    weights = wall_weights(discrete_speed_east, discrete_speed_north)
    table_rows = moment_table(discrete_speed_east, discrete_speed_north, discrete_speed_upward).T
    is_solid = solid_mask == 1

    def block_of(array, plane):
        start = (plane * plane_size).astype(jnp.int32)
        return lax.dynamic_slice_in_dim(array, start, plane_size, axis=array.ndim - 1)

    for time_step in range(STEPS):
        partial_value = jnp.dot(distribution.reshape(cells, NV), weights,
                          precision=lax.Precision.HIGHEST).reshape(GRID_ROWS_LEADING, GRID_COLS_TRAILING, 4)
        incoming = jnp.where(is_solid, neighbor_flux(partial_value, normal_code), 0.0)
        wall_rho = incoming / wall_norm
        current_field = distribution

        def moved_block(plane):
            current = block_of(current_field, plane)
            ghost_value = wall_rho[:, :, None] * block_of(shape_all, plane)
            ghosted = jnp.where(is_solid[:, :, None], ghost_value, current)
            moved = transport(ghosted, jnp.roll(ghosted, 1, 0), jnp.roll(ghosted, -1, 0),
                              jnp.roll(ghosted, 1, 1), jnp.roll(ghosted, -1, 1),
                              block_of(discrete_speed_east, plane), block_of(discrete_speed_north, plane))
            return moved, ghost_value

        def add_moments(plane, total):
            moved, unused = moved_block(plane)
            return total + jnp.dot(moved.reshape(cells, plane_size), block_of(table_rows, plane).T,
                                   precision=lax.Precision.HIGHEST)

        aggregated_integrals = lax.fori_loop(0, discrete_speed_total, add_moments, jnp.zeros((cells, 5), jnp.float32))

        def write_block(plane, result):
            moved, ghost_value = moved_block(plane)
            relaxed = relax_cells(moved.reshape(cells, plane_size), aggregated_integrals,
                                  block_of(discrete_speed_east, plane), block_of(discrete_speed_north, plane),
                                  block_of(discrete_speed_upward, plane), discrete_speed_total).reshape(GRID_ROWS_LEADING, GRID_COLS_TRAILING, plane_size)
            new_block = jnp.where(is_solid[:, :, None], ghost_value, relaxed)
            start = (plane * plane_size).astype(jnp.int32)
            return lax.dynamic_update_slice_in_dim(result, new_block, start, axis=2)

        distribution = lax.fori_loop(0, discrete_speed_total, write_block, jnp.zeros_like(current_field))
    return distribution
```

```python
import functools
import math

import jax
import jax.numpy as jnp
import ml_dtypes
import numpy as np
from jax import lax
from jax.experimental import pallas as pl
from jax.experimental.pallas import tpu as pltpu
from jax.sharding import PartitionSpec as P

NVEL = 16
STEPS = 3
SPAN = 12.0
COURANT = 0.08
INV_TAU = 2.0
WALL_T = 3.0
PLANE = NVEL * NVEL
LANES = 128
H = SPAN / NVEL
MESH = pl.DeviceIdType.MESH
F32 = jnp.float32
BF16 = jnp.bfloat16
HALVES = PLANE // LANES


def split3(x):
    x = np.asarray(x, np.float64)
    pieces = []
    for _ in range(3):
        piece = x.astype(np.float32).astype(ml_dtypes.bfloat16)
        pieces.append(piece)
        x = x - piece.astype(np.float64)
    return pieces


def tables(nz):
    axis = (np.arange(NVEL) - (NVEL - 1) / 2.0) * H
    vx = np.repeat(axis, NVEL)
    vy = np.tile(axis, NVEL)
    zloc = (np.arange(nz) - (nz - 1) / 2.0) * H
    lx, ly, lz = np.tile(vx, nz), np.tile(vy, nz), np.repeat(zloc, PLANE)

    def five(x, y, z):
        return [np.ones_like(x), x, y, z, x * x + y * y + z * z]

    def sides(x, y):
        return [np.maximum(x, 0), np.maximum(-x, 0), np.maximum(y, 0), np.maximum(-y, 0)]

    weight = np.zeros((40, nz * PLANE))
    for g, factor in enumerate([np.ones_like(lx)] + sides(lx, ly)):
        for r, phi in enumerate(five(lx, ly, lz)):
            weight[8 * g + r] = factor * phi
    w = np.concatenate(split3(weight), axis=0)

    norm = H**3 * (2 * math.pi * WALL_T) ** -1.5
    fx, fy, fz = np.tile(vx, NVEL), np.tile(vy, NVEL), np.repeat(axis, PLANE)
    shape = norm * np.exp(-(fx**2 + fy**2 + fz**2) / (2 * WALL_T))
    wall_norm = float(np.sum(shape * np.maximum(fx, 0)))
    wall = [
        [COURANT * float(np.sum(shape * s * phi)) for s in sides(fx, fy)]
        for phi in five(fx, fy, fz)
    ]

    cols = 2 + nz + 1 + 2
    b = np.zeros((16, cols * LANES))
    sxy = norm * np.exp(-(vx**2 + vy**2) / (2 * WALL_T))
    for half in range(2):
        ln = slice(half * LANES, (half + 1) * LANES)
        hx, hy = vx[ln], vy[ln]
        b[0, ln], b[1, ln], b[2, ln], b[3, ln] = 1.0, hx, hy, hx**2 + hy**2
        at = (3 + nz + half) * LANES
        to = slice(at, at + LANES)
        b[5 + nz, to] = COURANT * np.maximum(hx, 0) * sxy[ln]
        b[6 + nz, to] = COURANT * np.maximum(-hx, 0) * sxy[ln]
        b[7 + nz, to] = COURANT * np.maximum(hy, 0) * sxy[ln]
        b[8 + nz, to] = COURANT * np.maximum(-hy, 0) * sxy[ln]
    for z in range(nz + 1):
        b[4 + z, (2 + z) * LANES : (3 + z) * LANES] = 1.0
    bh, bm, bl = split3(b)
    bst = np.concatenate([bh, bm, bh, bl, bm, bh], axis=0)

    vec = np.zeros((8, LANES), np.float32)
    for half in range(2):
        ln = slice(half * LANES, (half + 1) * LANES)
        vec[half] = 1 - COURANT * (np.abs(vx[ln]) + np.abs(vy[ln]))
        vec[2 + half] = COURANT * np.abs(vx[ln])
    vec[4] = COURANT * np.abs(vy[:LANES])
    vec[5] = vy[:LANES] > 0
    return w, bst, vec, wall_norm, wall, norm


def kernel(
    cfg, f_hbm, masks, w_ref, b_ref, vec, out_hbm,
    fa, fb, bc, q, qy, qx, a_ref, r_ref, p_ref, pst, hs, hr, hb, wold,
    lsem, osem, zss, zrs, xss, xrs, hss, hrs, qyss, qyrs, qxss, qxrs,
):
    rows, cols, nz, nx, ny, nv, wall_norm, wall, norm = cfg
    cells = rows * cols
    chunk = 8
    cc = chunk * cols
    nch = rows // chunk
    gx, gy, vt = lax.axis_index("gx"), lax.axis_index("gy"), lax.axis_index("vert")
    right, left = {"gx": lax.rem(gx + 1, nx)}, {"gx": lax.rem(gx + nx - 1, nx)}
    across = [{"gy": lax.rem(gy + 1, ny)}]
    if ny > 2:
        across.append({"gy": lax.rem(gy + ny - 1, ny)})
    peers = [{"vert": lax.rem(vt + k, nv)} for k in range(1, nv)]

    def local_copy(k):
        return pltpu.make_async_copy(
            f_hbm.at[pl.ds(k * chunk, chunk)], fa.at[pl.ds(1 + k * chunk, chunk)], lsem.at[k]
        )

    for k in range(nch):
        local_copy(k).start()

    barrier = pltpu.get_barrier_semaphore()
    everyone = [right, left] + across + peers
    for dev in everyone:
        pl.semaphore_signal(barrier, inc=1, device_id=dev, device_id_type=MESH)
    pl.semaphore_wait(barrier, len(everyone))

    def remote(src, dst, ss, rs, dev):
        return pltpu.make_async_remote_copy(
            src_ref=src, dst_ref=dst, send_sem=ss, recv_sem=rs, device_id=dev, device_id_type=MESH
        )

    def halo_x(step, src, first, dst):
        out = []
        for z in range(nz):
            hi = pl.ds((2 * z + 1) * LANES, LANES)
            lo = pl.ds(2 * z * LANES, LANES)
            out.append(remote(src.at[first + rows - 1, :, hi], dst.at[0, :, hi],
                              xss.at[step, 0, z], xrs.at[step, 0, z], right))
            out.append(remote(src.at[first, :, lo], dst.at[rows + 1, :, lo],
                              xss.at[step, 1, z], xrs.at[step, 1, z], left))
        return out

    z0 = (vt.astype(F32) * nz + (nz - 1) / 2.0 - (NVEL - 1) / 2.0) * H
    vz = [z0 + (z - (nz - 1) / 2.0) * H for z in range(nz)]
    sz = [jnp.exp(jnp.full((1, LANES), 0.0, F32) - vz[z] * vz[z] / (2 * WALL_T)) for z in range(nz)]
    up = jnp.broadcast_to(vec[5:6, :], (8, LANES)) > 0.5
    sub = lax.broadcasted_iota(jnp.int32, (8, LANES), 0)
    edge_lo = up & (sub == 0)
    edge_hi = jnp.logical_not(up) & (sub == 7)

    def moments(x, k):
        hi = x.astype(BF16)
        lo = (x - hi.astype(F32)).astype(BF16)
        dims = (((1,), (1,)), ((), ()))
        o = lax.dot_general(w_ref[...], hi, dims, preferred_element_type=F32)
        o = o + lax.dot_general(w_ref[...], lo, dims, preferred_element_type=F32)
        at = pl.ds(pl.multiple_of(k * cc, cc), cc)
        q[:, at] = o[0:40] + o[40:80] + o[80:120]

    def pack(step, buf, k):
        for r in range(chunk):
            i = 1 + k * chunk + r
            for b in range(2 * nz):
                ln = slice(b * LANES, (b + 1) * LANES)
                hs[step, k, r : r + 1, ln] = jnp.where(
                    up[0:1], buf[i, cols - 1 : cols, ln], buf[i, 0:1, ln]
                )

    def load_chunk(k, carry):
        local_copy(k).wait()
        x = fa[pl.ds(1 + k * chunk, chunk)].reshape(cc, nz * PLANE)
        moments(x, k)
        at = pl.ds(pl.multiple_of(k * cc, cc), cc)
        ones = (lax.broadcasted_iota(jnp.int32, (8, LANES), 0) == 0).astype(BF16)
        gasb = lax.dot_general(masks[:, at].astype(BF16), ones, (((0,), (0,)), ((), ())),
                               preferred_element_type=F32)
        gasb = gasb.reshape(chunk, cols, LANES)
        for b in range(2 * nz):
            ln = slice(b * LANES, (b + 1) * LANES)
            fa[pl.ds(1 + k * chunk, chunk), :, ln] = fa[pl.ds(1 + k * chunk, chunk), :, ln] * gasb
        pack(0, fa, k)
        return carry

    xs = halo_x(0, f_hbm, 0, fa)
    for c in xs:
        c.start()
    lax.fori_loop(0, nch, load_chunk, 0)

    gas = masks[0:1, :]
    picks = [masks[1 + k : 2 + k, :] for k in range(4)]
    solid = masks[5:6, :] > 0.5
    lane = lax.broadcasted_iota(jnp.int32, (8, cells), 1)
    row8 = lax.broadcasted_iota(jnp.int32, (8, cells), 0)

    def shift(v, s):
        return pltpu.roll(v, s % cells, 1)

    wold[...] = jnp.zeros_like(wold)
    bufs = [fa, fb]
    for step in range(STEPS):
        src, dst = bufs[step % 2], bufs[(step + 1) % 2]
        last = step == STEPS - 1
        hcopy = [remote(hs.at[step], hr.at[step, n], hss.at[step, n], hrs.at[step, n], dev)
                 for n, dev in enumerate(across)]
        qcopy = [remote(q.at[pl.ds(24, 16)], qy.at[step, n], qyss.at[step, n], qyrs.at[step, n], dev)
                 for n, dev in enumerate(across)]
        qcopy += [
            remote(q.at[pl.ds(8, 8), pl.ds(cells - LANES, LANES)], qx.at[step, 0],
                   qxss.at[step, 0], qxrs.at[step, 0], right),
            remote(q.at[pl.ds(16, 8), pl.ds(0, LANES)], qx.at[step, 1],
                   qxss.at[step, 1], qxrs.at[step, 1], left),
        ]
        for c in qcopy:
            c.start()
        for c in hcopy:
            c.start()
        if step > 0:
            xs = halo_x(step, src, 1, src)
            for c in xs:
                c.start()

        xp, xm, yp, ym = (q[8 * g : 8 * g + 8, :] for g in range(1, 5))
        inc = (picks[0] * shift(xm[0:1], -cols) + picks[1] * shift(xp[0:1], cols)
               + picks[2] * shift(ym[0:1], -1) + picks[3] * shift(yp[0:1], 1))
        base = (q[0:8, :] - COURANT * (xp + xm + yp + ym)) * gas
        sxp, sxm = shift(xp * gas, cols), shift(xm * gas, -cols)
        syp, sym = shift(yp * gas, 1), shift(ym * gas, -1)
        for c in qcopy:
            c.wait()
        reps = cells // LANES
        left_in = jnp.concatenate([pltpu.roll(qx[step, 0], cols, 1)] * reps, axis=1)
        right_in = jnp.concatenate([pltpu.roll(qx[step, 1], LANES - cols, 1)] * reps, axis=1)
        sxp = jnp.where(lane < cols, left_in, sxp)
        sxm = jnp.where(lane >= cells - cols, right_in, sxm)
        col = lane % cols
        syp = jnp.where(col == 0, shift(qy[step, 0, 0:8], 1 - cols), syp)
        sym = jnp.where(col == cols - 1, shift(qy[step, len(across) - 1, 8:16], cols - 1), sym)
        part = base + COURANT * (sxp + sxm + syp + sym)
        z_row = part[3:4] + z0 * part[0:1]
        e_row = part[4:5] + 2 * z0 * part[3:4] + z0 * z0 * part[0:1]
        part = jnp.where(row8 == 3, z_row, jnp.where(row8 == 4, e_row, jnp.where(row8 == 5, inc, part)))
        a_ref[...] = part
        zc = [remote(a_ref, r_ref.at[step, k], zss.at[step, k], zrs.at[step, k], peers[k])
              for k in range(nv - 1)]
        for c in zc:
            c.start()
        for c in zc:
            c.wait()
        tot = part
        for k in range(nv - 1):
            tot = tot + r_ref[step, k]
        p_ref[0:8, :] = tot
        w = p_ref[5:6, :] * (1.0 / wall_norm)
        near = [shift(w, cols), shift(w, -cols), shift(w, 1), shift(w, -1)]
        mom = []
        for r in range(5):
            m = p_ref[r : r + 1, :]
            for d in range(4):
                if abs(wall[r][d]) > 1e-12 * abs(wall[0][0]):
                    m = m + wall[r][d] * near[d]
            mom.append(m)
        rho = mom[0]
        ux, uy, uz = mom[1] / rho, mom[2] / rho, mom[3] / rho
        temp = (mom[4] / rho - (ux * ux + uy * uy + uz * uz)) / 3.0
        rate = (INV_TAU / NVEL**3) * rho * jnp.exp(0.28 * jnp.log(temp))
        two_pi_t = (2.0 * math.pi) * temp
        amp = rate / (1.0 + rate) * rho * H**3 / (two_pi_t * jnp.sqrt(two_pi_t))
        inv = 1.0 / (1.0 + rate)
        ux, uy, uz = (jnp.where(solid, 0.0, v) for v in (ux, uy, uz))
        g = jnp.where(solid, 0.5 / WALL_T, 0.5 / temp)
        amp = jnp.where(solid, w * norm, amp)
        inv = jnp.where(solid, 0.0, inv)
        diff = w - wold[...]
        wold[...] = w
        lines = [-g * (ux * ux + uy * uy), 2 * g * ux, 2 * g * uy, -g]
        lines += [amp * jnp.exp(-g * (vz[z] - uz) * (vz[z] - uz)) for z in range(nz)]
        lines += [inv, shift(diff, cols), shift(diff, -cols), shift(diff, 1), shift(diff, -1)]
        lines += [jnp.zeros_like(inv)] * (16 - len(lines))
        for r in range(16):
            p_ref[r : r + 1, :] = lines[r]
        pv = p_ref[...]
        ph = pv.astype(BF16)
        rest = pv - ph.astype(F32)
        pm = rest.astype(BF16)
        plo = (rest - pm.astype(F32)).astype(BF16)
        for n, piece in enumerate([ph, ph, pm, ph, pm, plo]):
            pst[16 * n : 16 * n + 16, :] = piece

        for c in hcopy + xs:
            c.wait()

        def relax_row(i, rr, bcrow):
            def take(n):
                return bc[pl.ds(bcrow, cols), n * LANES : (n + 1) * LANES]

            inv_b = take(2 + nz)
            for half in range(2):
                exy = jnp.exp(take(half))
                pxy = take(3 + nz + half)
                for z in range(nz):
                    b = 2 * z + half
                    ln = slice(b * LANES, (b + 1) * LANES)
                    c = src[1 + i, :, ln]
                    r = src[i if half == 1 else i + 2, :, ln]
                    dn = pltpu.roll(c, 1, 0)
                    un = pltpu.roll(c, cols - 1, 0)
                    hrow = hb[rr, :, ln]
                    s = []
                    for t in range(cols // 8):
                        tl = slice(8 * t, 8 * t + 8)
                        v = jnp.where(up, dn[tl], un[tl])
                        if t == 0:
                            v = jnp.where(edge_lo, hrow, v)
                        if t == cols // 8 - 1:
                            v = jnp.where(edge_hi, hrow, v)
                        s.append(v)
                    s = jnp.concatenate(s, axis=0)
                    moved = c * vec[half : half + 1, :] + r * vec[2 + half : 3 + half, :] + s * vec[4:5, :]
                    dst[1 + i, :, ln] = inv_b * (moved + pxy * sz[z]) + take(2 + z) * exy

        def out_copy(k):
            return pltpu.make_async_copy(
                dst.at[pl.ds(1 + k * chunk, chunk)], out_hbm.at[pl.ds(k * chunk, chunk)], osem.at[k]
            )

        def relax_chunk(k, carry):
            at = pl.ds(pl.multiple_of(k * cc, cc), cc)
            bc[...] = lax.dot_general(pst[:, at], b_ref[...], (((0,), (0,)), ((), ())),
                                      preferred_element_type=F32)

            def one(r, c2):
                relax_row(k * chunk + r, r, pl.multiple_of(r * cols, cols))
                return c2

            for r in range(chunk):
                for b in range(2 * nz):
                    ln = slice(b * LANES, (b + 1) * LANES)
                    low = jnp.broadcast_to(hr[step, 0, k, r : r + 1, ln], (8, LANES))
                    if ny == 2:
                        hb[r, :, ln] = low
                    else:
                        high = jnp.broadcast_to(hr[step, 1, k, r : r + 1, ln], (8, LANES))
                        hb[r, :, ln] = jnp.where(up, low, high)

            lax.fori_loop(0, chunk, one, 0)
            if last:
                out_copy(k).start()
            else:
                pack(step + 1, dst, k)
                moments(dst[pl.ds(1 + k * chunk, chunk)].reshape(cc, nz * PLANE), k)
            return carry

        lax.fori_loop(0, nch, relax_chunk, 0)
        if last:
            for k in range(nch):
                out_copy(k).wait()


def solution(mesh):
    nx, ny, nv = mesh.shape["gx"], mesh.shape["gy"], mesh.shape["vert"]
    sides = 1 if ny == 2 else 2

    def on_device(f, solid_mask, normal_code):
        rows, cols, vel = f.shape
        nz = vel // PLANE
        cells = rows * cols
        w, bst, vec, wall_norm, wall, norm = tables(nz)
        sm = solid_mask.reshape(1, cells) == 1
        nc = normal_code.reshape(1, cells)
        lines = [jnp.logical_not(sm)] + [sm & (nc == k) for k in range(4)] + [sm]
        lines += [jnp.zeros_like(sm)] * 2
        masks = jnp.concatenate(lines, axis=0).astype(F32)
        cfg = (rows, cols, nz, nx, ny, nv, wall_norm, wall, norm)
        vm = pl.BlockSpec(memory_space=pltpu.VMEM)
        hbm = pl.BlockSpec(memory_space=pl.ANY)
        dma = pltpu.SemaphoreType.DMA
        bw = bst.shape[1]
        chunk = 8
        return pl.pallas_call(
            functools.partial(kernel, cfg),
            out_shape=jax.ShapeDtypeStruct(f.shape, F32),
            in_specs=[hbm, vm, vm, vm, vm],
            out_specs=hbm,
            scratch_shapes=[
                pltpu.VMEM((rows + 2, cols, vel), F32),
                pltpu.VMEM((rows + 2, cols, vel), F32),
                pltpu.VMEM((chunk * cols, bw), F32),
                pltpu.VMEM((40, cells), F32),
                pltpu.VMEM((STEPS, sides, 16, cells), F32),
                pltpu.VMEM((STEPS, 2, 8, LANES), F32),
                pltpu.VMEM((8, cells), F32),
                pltpu.VMEM((STEPS, nv - 1, 8, cells), F32),
                pltpu.VMEM((16, cells), F32),
                pltpu.VMEM((96, cells), BF16),
                pltpu.VMEM((STEPS, rows // chunk, chunk, vel), F32),
                pltpu.VMEM((STEPS, sides, rows // chunk, chunk, vel), F32),
                pltpu.VMEM((chunk, 8, vel), F32),
                pltpu.VMEM((1, cells), F32),
                dma((rows // chunk,)), dma((rows // chunk,)),
                dma((STEPS, nv - 1)), dma((STEPS, nv - 1)),
                dma((STEPS, 2, nz)), dma((STEPS, 2, nz)),
                dma((STEPS, sides)), dma((STEPS, sides)),
                dma((STEPS, sides)), dma((STEPS, sides)),
                dma((STEPS, 2)), dma((STEPS, 2)),
            ],
            compiler_params=pltpu.CompilerParams(
                collective_id=0, has_side_effects=True, vmem_limit_bytes=60 * 2**20
            ),
        )(f, masks, jnp.asarray(w), jnp.asarray(bst), jnp.asarray(vec))

    placed = (P("gx", "gy", "vert"), P("gx", "gy"), P("gx", "gy"))
    return jax.shard_map(
        on_device, mesh=mesh, in_specs=placed, out_specs=P("gx", "gy", "vert"), check_vma=False
    )
```

```python
import functools
import math

import jax
import jax.numpy as jnp
import ml_dtypes
import numpy as np
from jax import lax
from jax.experimental import pallas as pl
from jax.experimental.pallas import tpu as pltpu
from jax.sharding import PartitionSpec as P

NVEL = 16
STEPS = 3
SPAN = 12.0
COURANT = 0.08
INV_TAU = 2.0
WALL_T = 3.0
PLANE = NVEL * NVEL
LANES = 128
H = SPAN / NVEL
MESH = pl.DeviceIdType.MESH
F32 = jnp.float32
BF16 = jnp.bfloat16
HALVES = PLANE // LANES


def split3(x):
    x = np.asarray(x, np.float64)
    pieces = []
    for _ in range(3):
        piece = x.astype(np.float32).astype(ml_dtypes.bfloat16)
        pieces.append(piece)
        x = x - piece.astype(np.float64)
    return pieces


def tables(nz):
    axis = (np.arange(NVEL) - (NVEL - 1) / 2.0) * H
    vx = np.repeat(axis, NVEL)
    vy = np.tile(axis, NVEL)
    zloc = (np.arange(nz) - (nz - 1) / 2.0) * H
    lx, ly, lz = np.tile(vx, nz), np.tile(vy, nz), np.repeat(zloc, PLANE)

    def five(x, y, z):
        return [np.ones_like(x), x, y, z, x * x + y * y + z * z]

    def sides(x, y):
        return [np.maximum(x, 0), np.maximum(-x, 0), np.maximum(y, 0), np.maximum(-y, 0)]

    weight = np.zeros((40, nz * PLANE))
    for g, factor in enumerate([np.ones_like(lx)] + sides(lx, ly)):
        for r, phi in enumerate(five(lx, ly, lz)):
            weight[8 * g + r] = factor * phi
    w = np.concatenate(split3(weight), axis=0)

    norm = H**3 * (2 * math.pi * WALL_T) ** -1.5
    fx, fy, fz = np.tile(vx, NVEL), np.tile(vy, NVEL), np.repeat(axis, PLANE)
    shape = norm * np.exp(-(fx**2 + fy**2 + fz**2) / (2 * WALL_T))
    wall_norm = float(np.sum(shape * np.maximum(fx, 0)))
    wall = [
        [COURANT * float(np.sum(shape * s * phi)) for s in sides(fx, fy)]
        for phi in five(fx, fy, fz)
    ]

    cols = 2 + nz + 1 + 2
    b = np.zeros((16, cols * LANES))
    sxy = norm * np.exp(-(vx**2 + vy**2) / (2 * WALL_T))
    for half in range(2):
        ln = slice(half * LANES, (half + 1) * LANES)
        hx, hy = vx[ln], vy[ln]
        b[0, ln], b[1, ln], b[2, ln], b[3, ln] = 1.0, hx, hy, hx**2 + hy**2
        at = (3 + nz + half) * LANES
        to = slice(at, at + LANES)
        b[5 + nz, to] = COURANT * np.maximum(hx, 0) * sxy[ln]
        b[6 + nz, to] = COURANT * np.maximum(-hx, 0) * sxy[ln]
        b[7 + nz, to] = COURANT * np.maximum(hy, 0) * sxy[ln]
        b[8 + nz, to] = COURANT * np.maximum(-hy, 0) * sxy[ln]
    for z in range(nz + 1):
        b[4 + z, (2 + z) * LANES : (3 + z) * LANES] = 1.0
    bh, bm, bl = split3(b)
    bst = np.concatenate([bh, bm, bh, bl, bm, bh], axis=0)

    vec = np.zeros((8, LANES), np.float32)
    for half in range(2):
        ln = slice(half * LANES, (half + 1) * LANES)
        vec[half] = 1 - COURANT * (np.abs(vx[ln]) + np.abs(vy[ln]))
        vec[2 + half] = COURANT * np.abs(vx[ln])
    vec[4] = COURANT * np.abs(vy[:LANES])
    vec[5] = vy[:LANES] > 0
    return w, bst, vec, wall_norm, wall, norm


def lanes_of(vec):
    up = jnp.broadcast_to(vec[5:6, :], (8, LANES)) > 0.5
    sub = lax.broadcasted_iota(jnp.int32, (8, LANES), 0)
    return up, up & (sub == 0), jnp.logical_not(up) & (sub == 7)


def relax(geometry, src, dst, dst_first, pst, b_ref, vec, sz, hr, bc, halves, before, after, dot_rows):
    chunk, cols, nz, nch, sides = geometry
    cc = chunk * cols
    up, edge_lo, edge_hi = lanes_of(vec)

    def spread(k, slot):
        at = pl.ds(pl.multiple_of(k * cc, cc), cc)
        bc[slot] = lax.dot_general(pst[:, at], b_ref[...], (((0,), (0,)), ((), ())),
                                   preferred_element_type=F32)

    def rows_of(k, slot):
        for r in range(chunk):
            i = k * chunk + r

            def take(n):
                return bc[slot, r * cols : (r + 1) * cols, n * LANES : (n + 1) * LANES]

            inv_b = take(2 + nz)
            for half in range(2):
                exy = jnp.exp(take(half))
                pxy = take(3 + nz + half)
                for z in range(nz):
                    b = 2 * z + half
                    ln = slice(b * LANES, (b + 1) * LANES)
                    c = src[1 + i, :, ln]
                    side = src[i if half == 1 else i + 2, :, ln]
                    dn = pltpu.roll(c, 1, 0)
                    un = pltpu.roll(c, cols - 1, 0)
                    hrow = jnp.broadcast_to(hr[0, k, r : r + 1, ln], (8, LANES))
                    if sides == 2:
                        hrow = jnp.where(up, hrow, jnp.broadcast_to(hr[1, k, r : r + 1, ln], (8, LANES)))
                    s = []
                    for t in range(cols // 8):
                        tl = slice(8 * t, 8 * t + 8)
                        v = jnp.where(up, dn[tl], un[tl])
                        if t == 0:
                            v = jnp.where(edge_lo, hrow, v)
                        if t == cols // 8 - 1:
                            v = jnp.where(edge_hi, hrow, v)
                        s.append(v)
                    s = jnp.concatenate(s, axis=0)
                    moved = c * vec[half : half + 1, :] + side * vec[2 + half : 3 + half, :] + s * vec[4:5, :]
                    new = inv_b * (moved + pxy * sz[z]) + take(2 + z) * exy
                    dst[dst_first + i, :, ln] = new
                    if halves is not None:
                        hi = new.astype(BF16)
                        halves[slot, 0, r * cols : (r + 1) * cols, ln] = hi
                        halves[slot, 1, r * cols : (r + 1) * cols, ln] = (new - hi.astype(F32)).astype(BF16)

    spread(0, 0)

    def trip(m, carry):
        k = 2 * m
        before(k)
        spread(k + 1, 1)
        rows_of(k, 0)
        if dot_rows is not None:
            dot_rows(k, 0)
        before(k + 1)
        spread(lax.rem(k + 2, nch), 0)
        rows_of(k + 1, 1)
        if dot_rows is not None:
            dot_rows(k + 1, 1)
        after(k)
        after(k + 1)
        return carry

    lax.fori_loop(0, nch // 2, trip, 0)


def kernel(
    cfg, f_hbm, code, w_ref, b_ref, vec, f_mid, pst_out, hr_out, sz_out,
    fa, fb, bc, q, qy, qx, a_ref, r_ref, p_ref, pst, hs, hr, halves, wold, masks,
    lsem, osem, zss, zrs, xss, xrs, hss, hrs, qyss, qyrs, qxss, qxrs,
):
    rows, cols, nz, nx, ny, nv, wall_norm, wall, norm = cfg
    cells = rows * cols
    chunk = 8
    cc = chunk * cols
    nch = rows // chunk
    sides = 1 if ny == 2 else 2
    gx, gy, vt = lax.axis_index("gx"), lax.axis_index("gy"), lax.axis_index("vert")
    right, left = {"gx": lax.rem(gx + 1, nx)}, {"gx": lax.rem(gx + nx - 1, nx)}
    across = [{"gy": lax.rem(gy + 1, ny)}]
    if ny > 2:
        across.append({"gy": lax.rem(gy + ny - 1, ny)})
    peers = [{"vert": lax.rem(vt + k, nv)} for k in range(1, nv)]

    def local_copy(k):
        return pltpu.make_async_copy(
            f_hbm.at[pl.ds(k * chunk, chunk)], fa.at[pl.ds(1 + k * chunk, chunk)], lsem.at[k]
        )

    for k in range(nch):
        local_copy(k).start()

    barrier = pltpu.get_barrier_semaphore()
    everyone = [right, left] + across + peers
    for dev in everyone:
        pl.semaphore_signal(barrier, inc=1, device_id=dev, device_id_type=MESH)
    pl.semaphore_wait(barrier, len(everyone))

    def remote(src, dst, ss, rs, dev):
        return pltpu.make_async_remote_copy(
            src_ref=src, dst_ref=dst, send_sem=ss, recv_sem=rs, device_id=dev, device_id_type=MESH
        )

    def halo_x(step, src, first, dst):
        out = []
        for z in range(nz):
            hi = pl.ds((2 * z + 1) * LANES, LANES)
            lo = pl.ds(2 * z * LANES, LANES)
            out.append(remote(src.at[first + rows - 1, :, hi], dst.at[0, :, hi],
                              xss.at[step, 0, z], xrs.at[step, 0, z], right))
            out.append(remote(src.at[first, :, lo], dst.at[rows + 1, :, lo],
                              xss.at[step, 1, z], xrs.at[step, 1, z], left))
        return out

    z0 = (vt.astype(F32) * nz + (nz - 1) / 2.0 - (NVEL - 1) / 2.0) * H
    vz = [z0 + (z - (nz - 1) / 2.0) * H for z in range(nz)]
    sz = [jnp.exp(jnp.full((1, LANES), 0.0, F32) - vz[z] * vz[z] / (2 * WALL_T)) for z in range(nz)]
    up = lanes_of(vec)[0]

    def moments(hi, lo, k):
        dims = (((1,), (1,)), ((), ()))
        o = lax.dot_general(w_ref[...], hi, dims, preferred_element_type=F32)
        o = o + lax.dot_general(w_ref[...], lo, dims, preferred_element_type=F32)
        at = pl.ds(pl.multiple_of(k * cc, cc), cc)
        q[:, at] = o[0:40] + o[40:80] + o[80:120]

    def dot_rows(k, slot):
        moments(halves[slot, 0], halves[slot, 1], k)

    def mid_copy(buf, k):
        return pltpu.make_async_copy(
            buf.at[pl.ds(1 + k * chunk, chunk)], f_mid.at[pl.ds(1 + k * chunk, chunk)], osem.at[k]
        )

    def pack(step, buf, k):
        for r in range(chunk):
            i = 1 + k * chunk + r
            for b in range(2 * nz):
                ln = slice(b * LANES, (b + 1) * LANES)
                hs[step, k, r : r + 1, ln] = jnp.where(
                    up[0:1], buf[i, cols - 1 : cols, ln], buf[i, 0:1, ln]
                )

    def load_chunk(k, carry):
        local_copy(k).wait()
        x = fa[pl.ds(1 + k * chunk, chunk)].reshape(cc, nz * PLANE)
        hi = x.astype(BF16)
        moments(hi, (x - hi.astype(F32)).astype(BF16), k)
        at = pl.ds(pl.multiple_of(k * cc, cc), cc)
        ones = (lax.broadcasted_iota(jnp.int32, (8, LANES), 0) == 0).astype(BF16)
        gasb = lax.dot_general(masks[:, at].astype(BF16), ones, (((0,), (0,)), ((), ())),
                               preferred_element_type=F32)
        gasb = gasb.reshape(chunk, cols, LANES)
        for b in range(2 * nz):
            ln = slice(b * LANES, (b + 1) * LANES)
            fa[pl.ds(1 + k * chunk, chunk), :, ln] = fa[pl.ds(1 + k * chunk, chunk), :, ln] * gasb
        pack(0, fa, k)
        return carry

    flat = lax.broadcasted_iota(jnp.int32, (1, cells), 1)
    for n, on in enumerate([code[...] == 0] + [code[...] == k + 1 for k in range(4)]
                           + [code[...] > 0, flat % cols == 0, flat % cols == cols - 1]):
        masks[n : n + 1, :] = jnp.where(on, 1.0, 0.0)
    xs = halo_x(0, f_hbm, 0, fa)
    for c in xs:
        c.start()
    lax.fori_loop(0, nch, load_chunk, 0)

    first_col = masks[6:7, :] > 0.5
    last_col = masks[7:8, :] > 0.5
    gas = masks[0:1, :]
    picks = [masks[1 + k : 2 + k, :] for k in range(4)]
    solid = masks[5:6, :] > 0.5
    lane = lax.broadcasted_iota(jnp.int32, (8, cells), 1)
    row8 = lax.broadcasted_iota(jnp.int32, (8, cells), 0)

    def shift(v, s):
        return pltpu.roll(v, s % cells, 1)

    wold[...] = jnp.zeros_like(wold)
    bufs = [fa, fb]
    for step in range(STEPS):
        src, dst = bufs[step % 2], bufs[(step + 1) % 2]
        last = step == STEPS - 1
        hcopy = [remote(hs.at[step], hr.at[step, n], hss.at[step, n], hrs.at[step, n], dev)
                 for n, dev in enumerate(across)]
        qcopy = [remote(q.at[pl.ds(24, 16)], qy.at[step, n], qyss.at[step, n], qyrs.at[step, n], dev)
                 for n, dev in enumerate(across)]
        qcopy += [
            remote(q.at[pl.ds(8, 8), pl.ds(cells - LANES, LANES)], qx.at[step, 0],
                   qxss.at[step, 0], qxrs.at[step, 0], right),
            remote(q.at[pl.ds(16, 8), pl.ds(0, LANES)], qx.at[step, 1],
                   qxss.at[step, 1], qxrs.at[step, 1], left),
        ]
        for c in qcopy:
            c.start()
        for c in hcopy:
            c.start()
        if step > 0:
            xs = halo_x(step, src, 1, f_mid if last else src)
            for c in xs:
                c.start()

        xp, xm, yp, ym = (q[8 * g : 8 * g + 8, :] for g in range(1, 5))
        inc = (picks[0] * shift(xm[0:1], -cols) + picks[1] * shift(xp[0:1], cols)
               + picks[2] * shift(ym[0:1], -1) + picks[3] * shift(yp[0:1], 1))
        base = (q[0:8, :] - COURANT * (xp + xm + yp + ym)) * gas
        sxp, sxm = shift(xp * gas, cols), shift(xm * gas, -cols)
        syp, sym = shift(yp * gas, 1), shift(ym * gas, -1)
        for c in qcopy:
            c.wait()
        reps = cells // LANES
        left_in = jnp.concatenate([pltpu.roll(qx[step, 0], cols, 1)] * reps, axis=1)
        right_in = jnp.concatenate([pltpu.roll(qx[step, 1], LANES - cols, 1)] * reps, axis=1)
        sxp = jnp.where(lane < cols, left_in, sxp)
        sxm = jnp.where(lane >= cells - cols, right_in, sxm)
        syp = jnp.where(first_col, shift(qy[step, 0, 0:8], 1 - cols), syp)
        sym = jnp.where(last_col, shift(qy[step, len(across) - 1, 8:16], cols - 1), sym)
        part = base + COURANT * (sxp + sxm + syp + sym)
        z_row = part[3:4] + z0 * part[0:1]
        e_row = part[4:5] + 2 * z0 * part[3:4] + z0 * z0 * part[0:1]
        part = jnp.where(row8 == 3, z_row, jnp.where(row8 == 4, e_row, jnp.where(row8 == 5, inc, part)))
        a_ref[...] = part
        zc = [remote(a_ref, r_ref.at[step, k], zss.at[step, k], zrs.at[step, k], peers[k])
              for k in range(nv - 1)]
        for c in zc:
            c.start()
        for c in zc:
            c.wait()
        tot = part
        for k in range(nv - 1):
            tot = tot + r_ref[step, k]
        p_ref[0:8, :] = tot
        w = p_ref[5:6, :] * (1.0 / wall_norm)
        near = [shift(w, cols), shift(w, -cols), shift(w, 1), shift(w, -1)]
        mom = []
        for r in range(5):
            m = p_ref[r : r + 1, :]
            for d in range(4):
                if abs(wall[r][d]) > 1e-12 * abs(wall[0][0]):
                    m = m + wall[r][d] * near[d]
            mom.append(m)
        rho = mom[0]
        ux, uy, uz = mom[1] / rho, mom[2] / rho, mom[3] / rho
        temp = (mom[4] / rho - (ux * ux + uy * uy + uz * uz)) / 3.0
        rate = (INV_TAU / NVEL**3) * rho * jnp.exp(0.28 * jnp.log(temp))
        two_pi_t = (2.0 * math.pi) * temp
        amp = rate / (1.0 + rate) * rho * H**3 / (two_pi_t * jnp.sqrt(two_pi_t))
        inv = 1.0 / (1.0 + rate)
        ux, uy, uz = (jnp.where(solid, 0.0, v) for v in (ux, uy, uz))
        g = jnp.where(solid, 0.5 / WALL_T, 0.5 / temp)
        amp = jnp.where(solid, w * norm, amp)
        inv = jnp.where(solid, 0.0, inv)
        diff = w - wold[...]
        wold[...] = w
        lines = [-g * (ux * ux + uy * uy), 2 * g * ux, 2 * g * uy, -g]
        lines += [amp * jnp.exp(-g * (vz[z] - uz) * (vz[z] - uz)) for z in range(nz)]
        lines += [inv, shift(diff, cols), shift(diff, -cols), shift(diff, 1), shift(diff, -1)]
        lines += [jnp.zeros_like(inv)] * (16 - len(lines))
        for r in range(16):
            p_ref[r : r + 1, :] = lines[r]
        pv = p_ref[...]
        ph = pv.astype(BF16)
        rest = pv - ph.astype(F32)
        pm = rest.astype(BF16)
        plo = (rest - pm.astype(F32)).astype(BF16)
        for n, piece in enumerate([ph, ph, pm, ph, pm, plo]):
            pst[16 * n : 16 * n + 16, :] = piece

        for c in hcopy + xs:
            c.wait()
        if last:
            break

        def before(k):
            return None

        def after(k, step=step, dst=dst):
            pack(step + 1, dst, k)
            if step == STEPS - 2:
                mid_copy(dst, k).start()

        relax((chunk, cols, nz, nch, sides), src, dst, 1, pst, b_ref, vec, sz, hr.at[step],
              bc, halves, before, after, dot_rows)
    for k in range(nch):
        mid_copy(bufs[(STEPS - 1) % 2], k).wait()
    pst_out[...] = pst[...]
    hr_out[...] = hr[STEPS - 1]
    for z in range(nz):
        sz_out[z : z + 1, :] = sz[z]
    for z in range(nz, 8):
        sz_out[z : z + 1, :] = jnp.zeros((1, LANES), F32)


def finish(geometry, rows, f_mid, pst, hr, sz_ref, b_ref, vec, out_hbm, fa, fb, bc, lsem, osem):
    chunk, cols, nz, nch, sides = geometry

    def part(k):
        return pltpu.make_async_copy(
            f_mid.at[pl.ds(2 + k * chunk, chunk)], fa.at[pl.ds(2 + k * chunk, chunk)], lsem.at[k]
        )

    def out_copy(k):
        return pltpu.make_async_copy(
            fb.at[pl.ds(k * chunk, chunk)], out_hbm.at[pl.ds(k * chunk, chunk)], osem.at[k]
        )

    first = pltpu.make_async_copy(f_mid.at[pl.ds(0, 2)], fa.at[pl.ds(0, 2)], lsem.at[nch])
    first.start()
    for k in range(nch):
        part(k).start()
    first.wait()
    sz = [sz_ref[z : z + 1, :] for z in range(nz)]
    relax(geometry, fa, fb, 0, pst, b_ref, vec, sz, hr, bc, None,
          lambda k: part(k).wait(), lambda k: out_copy(k).start(), None)
    for k in range(nch):
        out_copy(k).wait()


def solution(mesh):
    nx, ny, nv = mesh.shape["gx"], mesh.shape["gy"], mesh.shape["vert"]
    sides = 1 if ny == 2 else 2

    def on_device(f, solid_mask, normal_code):
        rows, cols, vel = f.shape
        nz = vel // PLANE
        cells = rows * cols
        w, bst, vec, wall_norm, wall, norm = tables(nz)
        code = jnp.where(solid_mask == 1, normal_code + 1, 0).reshape(1, cells)
        nch = rows // 8
        geometry = (8, cols, nz, nch, sides)
        cfg = (rows, cols, nz, nx, ny, nv, wall_norm, wall, norm)
        vm = pl.BlockSpec(memory_space=pltpu.VMEM)
        hbm = pl.BlockSpec(memory_space=pl.ANY)
        dma = pltpu.SemaphoreType.DMA
        bw = bst.shape[1]
        chunk = 8
        bst, vec = jnp.asarray(bst), jnp.asarray(vec)
        f_mid, pst, hr, sz = pl.pallas_call(
            functools.partial(kernel, cfg),
            out_shape=[
                jax.ShapeDtypeStruct((rows + 2, cols, vel), F32),
                jax.ShapeDtypeStruct((96, cells), BF16),
                jax.ShapeDtypeStruct((sides, nch, chunk, vel), F32),
                jax.ShapeDtypeStruct((8, LANES), F32),
            ],
            in_specs=[hbm, vm, vm, vm, vm],
            out_specs=[pl.BlockSpec(memory_space=pltpu.HBM), vm, vm, vm],
            scratch_shapes=[
                pltpu.VMEM((rows + 2, cols, vel), F32),
                pltpu.VMEM((rows + 2, cols, vel), F32),
                pltpu.VMEM((2, chunk * cols, bw), F32),
                pltpu.VMEM((40, cells), F32),
                pltpu.VMEM((STEPS, sides, 16, cells), F32),
                pltpu.VMEM((STEPS, 2, 8, LANES), F32),
                pltpu.VMEM((8, cells), F32),
                pltpu.VMEM((STEPS, nv - 1, 8, cells), F32),
                pltpu.VMEM((16, cells), F32),
                pltpu.VMEM((96, cells), BF16),
                pltpu.VMEM((STEPS, rows // chunk, chunk, vel), F32),
                pltpu.VMEM((STEPS, sides, rows // chunk, chunk, vel), F32),
                pltpu.VMEM((2, 2, chunk * cols, vel), BF16),
                pltpu.VMEM((1, cells), F32),
                pltpu.VMEM((8, cells), F32),
                dma((rows // chunk,)), dma((rows // chunk,)),
                dma((STEPS, nv - 1)), dma((STEPS, nv - 1)),
                dma((STEPS, 2, nz)), dma((STEPS, 2, nz)),
                dma((STEPS, sides)), dma((STEPS, sides)),
                dma((STEPS, sides)), dma((STEPS, sides)),
                dma((STEPS, 2)), dma((STEPS, 2)),
            ],
            compiler_params=pltpu.CompilerParams(
                collective_id=0, has_side_effects=True, vmem_limit_bytes=60 * 2**20
            ),
        )(f, code, jnp.asarray(w), bst, vec)
        return pl.pallas_call(
            functools.partial(finish, geometry, rows),
            out_shape=jax.ShapeDtypeStruct(f.shape, F32),
            in_specs=[pl.BlockSpec(memory_space=pltpu.HBM), vm, vm, vm, vm, vm],
            out_specs=hbm,
            scratch_shapes=[
                pltpu.VMEM((rows + 2, cols, vel), F32),
                pltpu.VMEM((rows, cols, vel), F32),
                pltpu.VMEM((2, chunk * cols, bw), F32),
                dma((nch + 1,)), dma((nch,)),
            ],
            compiler_params=pltpu.CompilerParams(vmem_limit_bytes=60 * 2**20),
        )(f_mid, pst, hr, sz, bst, vec)

    placed = (P("gx", "gy", "vert"), P("gx", "gy"), P("gx", "gy"))
    return jax.shard_map(
        on_device, mesh=mesh, in_specs=placed, out_specs=P("gx", "gy", "vert"), check_vma=False
    )
```

```python
import functools
import math

import jax
import jax.numpy as jnp
import ml_dtypes
import numpy as np
from jax import lax
from jax.experimental import pallas as pl
from jax.experimental.pallas import tpu as pltpu
from jax.sharding import PartitionSpec as P

NVEL = 16
STEPS = 3
SPAN = 12.0
COURANT = 0.08
INV_TAU = 2.0
WALL_T = 3.0
PLANE = NVEL * NVEL
LANES = 128
H = SPAN / NVEL
MESH = pl.DeviceIdType.MESH
F32 = jnp.float32
BF16 = jnp.bfloat16
HALVES = PLANE // LANES


def split3(x):
    x = np.asarray(x, np.float64)
    pieces = []
    for _ in range(3):
        piece = x.astype(np.float32).astype(ml_dtypes.bfloat16)
        pieces.append(piece)
        x = x - piece.astype(np.float64)
    return pieces


def tables(nz):
    axis = (np.arange(NVEL) - (NVEL - 1) / 2.0) * H
    vx = np.repeat(axis, NVEL)
    vy = np.tile(axis, NVEL)
    zloc = (np.arange(nz) - (nz - 1) / 2.0) * H
    lx, ly, lz = np.tile(vx, nz), np.tile(vy, nz), np.repeat(zloc, PLANE)

    def five(x, y, z):
        return [np.ones_like(x), x, y, z, x * x + y * y + z * z]

    def sides(x, y):
        return [np.maximum(x, 0), np.maximum(-x, 0), np.maximum(y, 0), np.maximum(-y, 0)]

    weight = np.zeros((40, nz * PLANE))
    for g, factor in enumerate([np.ones_like(lx)] + sides(lx, ly)):
        for r, phi in enumerate(five(lx, ly, lz)):
            weight[8 * g + r] = factor * phi
    w = np.concatenate(split3(weight), axis=0)

    norm = H**3 * (2 * math.pi * WALL_T) ** -1.5
    fx, fy, fz = np.tile(vx, NVEL), np.tile(vy, NVEL), np.repeat(axis, PLANE)
    shape = norm * np.exp(-(fx**2 + fy**2 + fz**2) / (2 * WALL_T))
    wall_norm = float(np.sum(shape * np.maximum(fx, 0)))
    wall = [
        [COURANT * float(np.sum(shape * s * phi)) for s in sides(fx, fy)]
        for phi in five(fx, fy, fz)
    ]

    cols = 2 + nz + 1 + 2
    b = np.zeros((16, cols * LANES))
    sxy = norm * np.exp(-(vx**2 + vy**2) / (2 * WALL_T))
    for half in range(2):
        ln = slice(half * LANES, (half + 1) * LANES)
        hx, hy = vx[ln], vy[ln]
        b[0, ln], b[1, ln], b[2, ln], b[3, ln] = 1.0, hx, hy, hx**2 + hy**2
        at = (3 + nz + half) * LANES
        to = slice(at, at + LANES)
        b[5 + nz, to] = COURANT * np.maximum(hx, 0) * sxy[ln]
        b[6 + nz, to] = COURANT * np.maximum(-hx, 0) * sxy[ln]
        b[7 + nz, to] = COURANT * np.maximum(hy, 0) * sxy[ln]
        b[8 + nz, to] = COURANT * np.maximum(-hy, 0) * sxy[ln]
    for z in range(nz + 1):
        b[4 + z, (2 + z) * LANES : (3 + z) * LANES] = 1.0
    bh, bm, bl = split3(b)
    bst = np.concatenate([bh, bm, bh, bl, bm, bh], axis=0)

    vec = np.zeros((8, LANES), np.float32)
    for half in range(2):
        ln = slice(half * LANES, (half + 1) * LANES)
        vec[half] = 1 - COURANT * (np.abs(vx[ln]) + np.abs(vy[ln]))
        vec[2 + half] = COURANT * np.abs(vx[ln])
    vec[4] = COURANT * np.abs(vy[:LANES])
    vec[5] = vy[:LANES] > 0
    return w, bst, vec, wall_norm, wall, norm


def lanes_of(vec):
    up = jnp.broadcast_to(vec[5:6, :], (8, LANES)) > 0.5
    sub = lax.broadcasted_iota(jnp.int32, (8, LANES), 0)
    return up, up & (sub == 0), jnp.logical_not(up) & (sub == 7)


def relax(geometry, src, dst, dst_first, pst, b_ref, vec, sz, hr, bc, halves, before, after, dot_rows):
    chunk, cols, nz, nch, sides = geometry
    cc = chunk * cols
    up, edge_lo, edge_hi = lanes_of(vec)

    def spread(k, slot):
        at = pl.ds(pl.multiple_of(k * cc, cc), cc)
        bc[slot] = lax.dot_general(pst[:, at], b_ref[...], (((0,), (0,)), ((), ())),
                                   preferred_element_type=F32)

    def rows_of(k, slot):
        for r in range(chunk):
            i = k * chunk + r

            def take(n):
                return bc[slot, r * cols : (r + 1) * cols, n * LANES : (n + 1) * LANES]

            inv_b = take(2 + nz)
            for half in range(2):
                exy = jnp.exp(take(half))
                pxy = take(3 + nz + half)
                for z in range(nz):
                    b = 2 * z + half
                    ln = slice(b * LANES, (b + 1) * LANES)
                    c = src[1 + i, :, ln]
                    side = src[i if half == 1 else i + 2, :, ln]
                    dn = pltpu.roll(c, 1, 0)
                    un = pltpu.roll(c, cols - 1, 0)
                    hrow = jnp.broadcast_to(hr[0, k, r : r + 1, ln], (8, LANES))
                    if sides == 2:
                        hrow = jnp.where(up, hrow, jnp.broadcast_to(hr[1, k, r : r + 1, ln], (8, LANES)))
                    s = []
                    for t in range(cols // 8):
                        tl = slice(8 * t, 8 * t + 8)
                        v = jnp.where(up, dn[tl], un[tl])
                        if t == 0:
                            v = jnp.where(edge_lo, hrow, v)
                        if t == cols // 8 - 1:
                            v = jnp.where(edge_hi, hrow, v)
                        s.append(v)
                    s = jnp.concatenate(s, axis=0)
                    moved = c * vec[half : half + 1, :] + side * vec[2 + half : 3 + half, :] + s * vec[4:5, :]
                    new = inv_b * (moved + pxy * sz[z]) + take(2 + z) * exy
                    dst[dst_first + i, :, ln] = new
                    if halves is not None:
                        hi = new.astype(BF16)
                        halves[slot, 0, r * cols : (r + 1) * cols, ln] = hi
                        halves[slot, 1, r * cols : (r + 1) * cols, ln] = (new - hi.astype(F32)).astype(BF16)

    spread(0, 0)

    def trip(m, carry):
        k = 2 * m
        before(k)
        spread(k + 1, 1)
        rows_of(k, 0)
        if dot_rows is not None:
            dot_rows(k, 0)
        before(k + 1)
        spread(lax.rem(k + 2, nch), 0)
        rows_of(k + 1, 1)
        if dot_rows is not None:
            dot_rows(k + 1, 1)
        after(k)
        after(k + 1)
        return carry

    lax.fori_loop(0, nch // 2, trip, 0)


def kernel(
    cfg, f_hbm, code, w_ref, b_ref, vec, f_mid, pst_out, hr_out, sz_out,
    fa, fb, bc, q, qy, qx, a_ref, r_ref, p_ref, pst, hs, hr, halves, wold, masks,
    lsem, osem, zss, zrs, xss, xrs, hss, hrs, qyss, qyrs, qxss, qxrs,
):
    rows, cols, nz, nx, ny, nv, wall_norm, wall, norm = cfg
    cells = rows * cols
    chunk = 8
    cc = chunk * cols
    nch = rows // chunk
    sides = 1 if ny == 2 else 2
    gx, gy, vt = lax.axis_index("gx"), lax.axis_index("gy"), lax.axis_index("vert")
    right, left = {"gx": lax.rem(gx + 1, nx)}, {"gx": lax.rem(gx + nx - 1, nx)}
    across = [{"gy": lax.rem(gy + 1, ny)}]
    if ny > 2:
        across.append({"gy": lax.rem(gy + ny - 1, ny)})
    peers = [{"vert": lax.rem(vt + k, nv)} for k in range(1, nv)]

    def local_copy(k):
        return pltpu.make_async_copy(
            f_hbm.at[pl.ds(k * chunk, chunk)], fa.at[pl.ds(1 + k * chunk, chunk)], lsem.at[k]
        )

    for k in range(nch):
        local_copy(k).start()

    barrier = pltpu.get_barrier_semaphore()
    everyone = [right, left] + across + peers
    for dev in everyone:
        pl.semaphore_signal(barrier, inc=1, device_id=dev, device_id_type=MESH)
    pl.semaphore_wait(barrier, len(everyone))

    def remote(src, dst, ss, rs, dev):
        return pltpu.make_async_remote_copy(
            src_ref=src, dst_ref=dst, send_sem=ss, recv_sem=rs, device_id=dev, device_id_type=MESH
        )

    def halo_x(step, src, first, dst):
        out = []
        for z in range(nz):
            hi = pl.ds((2 * z + 1) * LANES, LANES)
            lo = pl.ds(2 * z * LANES, LANES)
            out.append(remote(src.at[first + rows - 1, :, hi], dst.at[0, :, hi],
                              xss.at[step, 0, z], xrs.at[step, 0, z], right))
            out.append(remote(src.at[first, :, lo], dst.at[rows + 1, :, lo],
                              xss.at[step, 1, z], xrs.at[step, 1, z], left))
        return out

    z0 = (vt.astype(F32) * nz + (nz - 1) / 2.0 - (NVEL - 1) / 2.0) * H
    vz = [z0 + (z - (nz - 1) / 2.0) * H for z in range(nz)]
    sz = [jnp.exp(jnp.full((1, LANES), 0.0, F32) - vz[z] * vz[z] / (2 * WALL_T)) for z in range(nz)]
    up = lanes_of(vec)[0]

    def moments(hi, lo, k):
        dims = (((1,), (1,)), ((), ()))
        o = lax.dot_general(w_ref[...], hi, dims, preferred_element_type=F32)
        o = o + lax.dot_general(w_ref[...], lo, dims, preferred_element_type=F32)
        at = pl.ds(pl.multiple_of(k * cc, cc), cc)
        q[:, at] = o[0:40] + o[40:80] + o[80:120]

    def dot_rows(k, slot):
        moments(halves[slot, 0], halves[slot, 1], k)

    def mid_copy(buf, k):
        return pltpu.make_async_copy(
            buf.at[pl.ds(1 + k * chunk, chunk)], f_mid.at[pl.ds(1 + k * chunk, chunk)], osem.at[k]
        )

    def pack(step, buf, k):
        for r in range(chunk):
            i = 1 + k * chunk + r
            for b in range(2 * nz):
                ln = slice(b * LANES, (b + 1) * LANES)
                hs[step, k, r : r + 1, ln] = jnp.where(
                    up[0:1], buf[i, cols - 1 : cols, ln], buf[i, 0:1, ln]
                )

    def load_chunk(k, carry):
        local_copy(k).wait()
        x = fa[pl.ds(1 + k * chunk, chunk)].reshape(cc, nz * PLANE)
        hi = x.astype(BF16)
        moments(hi, (x - hi.astype(F32)).astype(BF16), k)
        at = pl.ds(pl.multiple_of(k * cc, cc), cc)
        ones = (lax.broadcasted_iota(jnp.int32, (8, LANES), 0) == 0).astype(BF16)
        gasb = lax.dot_general(masks[:, at].astype(BF16), ones, (((0,), (0,)), ((), ())),
                               preferred_element_type=F32)
        gasb = gasb.reshape(chunk, cols, LANES)
        for b in range(2 * nz):
            ln = slice(b * LANES, (b + 1) * LANES)
            fa[pl.ds(1 + k * chunk, chunk), :, ln] = fa[pl.ds(1 + k * chunk, chunk), :, ln] * gasb
        pack(0, fa, k)
        return carry

    flat = lax.broadcasted_iota(jnp.int32, (1, cells), 1)
    for n, on in enumerate([code[...] == 0] + [code[...] == k + 1 for k in range(4)]
                           + [code[...] > 0, flat % cols == 0, flat % cols == cols - 1]):
        masks[n : n + 1, :] = jnp.where(on, 1.0, 0.0)
    xs = halo_x(0, f_hbm, 0, fa)
    for c in xs:
        c.start()
    lax.fori_loop(0, nch, load_chunk, 0)

    first_col = masks[6:7, :] > 0.5
    last_col = masks[7:8, :] > 0.5
    gas = masks[0:1, :]
    picks = [masks[1 + k : 2 + k, :] for k in range(4)]
    solid = masks[5:6, :] > 0.5
    lane = lax.broadcasted_iota(jnp.int32, (8, cells), 1)
    row8 = lax.broadcasted_iota(jnp.int32, (8, cells), 0)

    def shift(v, s):
        return pltpu.roll(v, s % cells, 1)

    wold[...] = jnp.zeros_like(wold)
    bufs = [fa, fb]
    for step in range(STEPS):
        src, dst = bufs[step % 2], bufs[(step + 1) % 2]
        last = step == STEPS - 1
        hcopy = [remote(hs.at[step], hr.at[step, n], hss.at[step, n], hrs.at[step, n], dev)
                 for n, dev in enumerate(across)]
        qcopy = [remote(q.at[pl.ds(24, 16)], qy.at[step, n], qyss.at[step, n], qyrs.at[step, n], dev)
                 for n, dev in enumerate(across)]
        qcopy += [
            remote(q.at[pl.ds(8, 8), pl.ds(cells - LANES, LANES)], qx.at[step, 0],
                   qxss.at[step, 0], qxrs.at[step, 0], right),
            remote(q.at[pl.ds(16, 8), pl.ds(0, LANES)], qx.at[step, 1],
                   qxss.at[step, 1], qxrs.at[step, 1], left),
        ]
        for c in qcopy:
            c.start()
        for c in hcopy:
            c.start()
        if step > 0:
            xs = halo_x(step, src, 1, f_mid if last else src)
            for c in xs:
                c.start()

        xp, xm, yp, ym = (q[8 * g : 8 * g + 8, :] for g in range(1, 5))
        inc = (picks[0] * shift(xm[0:1], -cols) + picks[1] * shift(xp[0:1], cols)
               + picks[2] * shift(ym[0:1], -1) + picks[3] * shift(yp[0:1], 1))
        base = (q[0:8, :] - COURANT * (xp + xm + yp + ym)) * gas
        sxp, sxm = shift(xp * gas, cols), shift(xm * gas, -cols)
        syp, sym = shift(yp * gas, 1), shift(ym * gas, -1)
        for c in qcopy:
            c.wait()
        reps = cells // LANES
        left_in = jnp.concatenate([pltpu.roll(qx[step, 0], cols, 1)] * reps, axis=1)
        right_in = jnp.concatenate([pltpu.roll(qx[step, 1], LANES - cols, 1)] * reps, axis=1)
        sxp = jnp.where(lane < cols, left_in, sxp)
        sxm = jnp.where(lane >= cells - cols, right_in, sxm)
        syp = jnp.where(first_col, shift(qy[step, 0, 0:8], 1 - cols), syp)
        sym = jnp.where(last_col, shift(qy[step, len(across) - 1, 8:16], cols - 1), sym)
        part = base + COURANT * (sxp + sxm + syp + sym)
        z_row = part[3:4] + z0 * part[0:1]
        e_row = part[4:5] + 2 * z0 * part[3:4] + z0 * z0 * part[0:1]
        part = jnp.where(row8 == 3, z_row, jnp.where(row8 == 4, e_row, jnp.where(row8 == 5, inc, part)))
        a_ref[...] = part
        zc = [remote(a_ref.at[pl.ds(0, 6)], r_ref.at[step, k, pl.ds(0, 6)], zss.at[step, k], zrs.at[step, k], peers[k])
              for k in range(nv - 1)]
        for c in zc:
            c.start()
        for c in zc:
            c.wait()
        tot = part[0:6]
        for k in range(nv - 1):
            tot = tot + r_ref[step, k, 0:6]
        p_ref[0:6, :] = tot
        w = p_ref[5:6, :] * (1.0 / wall_norm)
        near = [shift(w, cols), shift(w, -cols), shift(w, 1), shift(w, -1)]
        mom = []
        for r in range(5):
            m = p_ref[r : r + 1, :]
            for d in range(4):
                if abs(wall[r][d]) > 1e-12 * abs(wall[0][0]):
                    m = m + wall[r][d] * near[d]
            mom.append(m)
        rho = mom[0]
        ux, uy, uz = mom[1] / rho, mom[2] / rho, mom[3] / rho
        temp = (mom[4] / rho - (ux * ux + uy * uy + uz * uz)) / 3.0
        rate = (INV_TAU / NVEL**3) * rho * jnp.exp(0.28 * jnp.log(temp))
        two_pi_t = (2.0 * math.pi) * temp
        amp = rate / (1.0 + rate) * rho * H**3 / (two_pi_t * jnp.sqrt(two_pi_t))
        inv = 1.0 / (1.0 + rate)
        ux, uy, uz = (jnp.where(solid, 0.0, v) for v in (ux, uy, uz))
        g = jnp.where(solid, 0.5 / WALL_T, 0.5 / temp)
        amp = jnp.where(solid, w * norm, amp)
        inv = jnp.where(solid, 0.0, inv)
        diff = w - wold[...]
        wold[...] = w
        lines = [-g * (ux * ux + uy * uy), 2 * g * ux, 2 * g * uy, -g]
        lines += [amp * jnp.exp(-g * (vz[z] - uz) * (vz[z] - uz)) for z in range(nz)]
        lines += [inv, shift(diff, cols), shift(diff, -cols), shift(diff, 1), shift(diff, -1)]
        lines += [jnp.zeros_like(inv)] * (16 - len(lines))
        for r in range(16):
            p_ref[r : r + 1, :] = lines[r]
        pv = p_ref[...]
        ph = pv.astype(BF16)
        rest = pv - ph.astype(F32)
        pm = rest.astype(BF16)
        plo = (rest - pm.astype(F32)).astype(BF16)
        for n, piece in enumerate([ph, ph, pm, ph, pm, plo]):
            pst[16 * n : 16 * n + 16, :] = piece

        for c in hcopy + xs:
            c.wait()
        if last:
            break

        def before(k):
            return None

        def after(k, step=step, dst=dst):
            pack(step + 1, dst, k)
            if step == STEPS - 2:
                mid_copy(dst, k).start()

        relax((chunk, cols, nz, nch, sides), src, dst, 1, pst, b_ref, vec, sz, hr.at[step],
              bc, halves, before, after, dot_rows)
    for k in range(nch):
        mid_copy(bufs[(STEPS - 1) % 2], k).wait()
    pst_out[...] = pst[...]
    hr_out[...] = hr[STEPS - 1]
    for z in range(nz):
        sz_out[z : z + 1, :] = sz[z]
    for z in range(nz, 8):
        sz_out[z : z + 1, :] = jnp.zeros((1, LANES), F32)


def finish(geometry, rows, f_mid, pst, hr, sz_ref, b_ref, vec, out_hbm, fa, fb, bc, lsem, osem):
    chunk, cols, nz, nch, sides = geometry

    def part(k):
        return pltpu.make_async_copy(
            f_mid.at[pl.ds(2 + k * chunk, chunk)], fa.at[pl.ds(2 + k * chunk, chunk)], lsem.at[k]
        )

    def out_copy(k):
        return pltpu.make_async_copy(
            fb.at[pl.ds(k * chunk, chunk)], out_hbm.at[pl.ds(k * chunk, chunk)], osem.at[k]
        )

    first = pltpu.make_async_copy(f_mid.at[pl.ds(0, 2)], fa.at[pl.ds(0, 2)], lsem.at[nch])
    first.start()
    for k in range(nch):
        part(k).start()
    first.wait()
    sz = [sz_ref[z : z + 1, :] for z in range(nz)]
    relax(geometry, fa, fb, 0, pst, b_ref, vec, sz, hr, bc, None,
          lambda k: part(k).wait(), lambda k: out_copy(k).start(), None)
    for k in range(nch):
        out_copy(k).wait()


def solution(mesh):
    nx, ny, nv = mesh.shape["gx"], mesh.shape["gy"], mesh.shape["vert"]
    sides = 1 if ny == 2 else 2

    def on_device(f, solid_mask, normal_code):
        rows, cols, vel = f.shape
        nz = vel // PLANE
        cells = rows * cols
        w, bst, vec, wall_norm, wall, norm = tables(nz)
        code = jnp.where(solid_mask == 1, normal_code + 1, 0).reshape(1, cells)
        nch = rows // 8
        geometry = (8, cols, nz, nch, sides)
        cfg = (rows, cols, nz, nx, ny, nv, wall_norm, wall, norm)
        vm = pl.BlockSpec(memory_space=pltpu.VMEM)
        hbm = pl.BlockSpec(memory_space=pl.ANY)
        dma = pltpu.SemaphoreType.DMA
        bw = bst.shape[1]
        chunk = 8
        bst, vec = jnp.asarray(bst), jnp.asarray(vec)
        f_mid, pst, hr, sz = pl.pallas_call(
            functools.partial(kernel, cfg),
            out_shape=[
                jax.ShapeDtypeStruct((rows + 2, cols, vel), F32),
                jax.ShapeDtypeStruct((96, cells), BF16),
                jax.ShapeDtypeStruct((sides, nch, chunk, vel), F32),
                jax.ShapeDtypeStruct((8, LANES), F32),
            ],
            in_specs=[hbm, vm, vm, vm, vm],
            out_specs=[pl.BlockSpec(memory_space=pltpu.HBM), vm, vm, vm],
            scratch_shapes=[
                pltpu.VMEM((rows + 2, cols, vel), F32),
                pltpu.VMEM((rows + 2, cols, vel), F32),
                pltpu.VMEM((2, chunk * cols, bw), F32),
                pltpu.VMEM((40, cells), F32),
                pltpu.VMEM((STEPS, sides, 16, cells), F32),
                pltpu.VMEM((STEPS, 2, 8, LANES), F32),
                pltpu.VMEM((8, cells), F32),
                pltpu.VMEM((STEPS, nv - 1, 8, cells), F32),
                pltpu.VMEM((16, cells), F32),
                pltpu.VMEM((96, cells), BF16),
                pltpu.VMEM((STEPS, rows // chunk, chunk, vel), F32),
                pltpu.VMEM((STEPS, sides, rows // chunk, chunk, vel), F32),
                pltpu.VMEM((2, 2, chunk * cols, vel), BF16),
                pltpu.VMEM((1, cells), F32),
                pltpu.VMEM((8, cells), F32),
                dma((rows // chunk,)), dma((rows // chunk,)),
                dma((STEPS, nv - 1)), dma((STEPS, nv - 1)),
                dma((STEPS, 2, nz)), dma((STEPS, 2, nz)),
                dma((STEPS, sides)), dma((STEPS, sides)),
                dma((STEPS, sides)), dma((STEPS, sides)),
                dma((STEPS, 2)), dma((STEPS, 2)),
            ],
            compiler_params=pltpu.CompilerParams(
                collective_id=0, has_side_effects=True, vmem_limit_bytes=60 * 2**20
            ),
        )(f, code, jnp.asarray(w), bst, vec)
        return pl.pallas_call(
            functools.partial(finish, geometry, rows),
            out_shape=jax.ShapeDtypeStruct(f.shape, F32),
            in_specs=[pl.BlockSpec(memory_space=pltpu.HBM), vm, vm, vm, vm, vm],
            out_specs=hbm,
            scratch_shapes=[
                pltpu.VMEM((rows + 2, cols, vel), F32),
                pltpu.VMEM((rows, cols, vel), F32),
                pltpu.VMEM((2, chunk * cols, bw), F32),
                dma((nch + 1,)), dma((nch,)),
            ],
            compiler_params=pltpu.CompilerParams(vmem_limit_bytes=60 * 2**20),
        )(f_mid, pst, hr, sz, bst, vec)

    placed = (P("gx", "gy", "vert"), P("gx", "gy"), P("gx", "gy"))
    return jax.shard_map(
        on_device, mesh=mesh, in_specs=placed, out_specs=P("gx", "gy", "vert"), check_vma=False
    )
```
